32 devices in a mesh: seq: 8 (over z, x), head: 2 (over y), enc: 2 (over core).
Axes of the slice: x: 2, y: 2, z: 4, core: 2. Of those that a mesh axis runs over, the one named last changes fastest.
Arguments:
- queries: bfloat16 [2560, 1024], P('seq', ('head', 'enc')), may hold values from -2000 to 2000
- keys: bfloat16 [2560, 1024], P('seq', ('head', 'enc')), may hold values from -2000 to 2000
- values: bfloat16 [2560, 1024], P('seq', ('head', 'enc')), may hold values from -6 to 6
- out_weight: bfloat16 [1024, 5120], P(('head', 'enc'), 'seq'), may hold values from -0.25 to 0.25
- q_gain: float32 [1024], P(('head', 'enc')), may hold values from 0.75 to 3
- k_gain: float32 [1024], P(('head', 'enc')), may hold values from 0.75 to 3
- gate: float32 [5120], P(('head', 'enc')), may hold values from 1 to 8
- valid_count: int32 [1], replicated, may hold values from 1280 to 2560
Outputs:
- update: bfloat16 [2560, 5120], P('seq', ('head', 'enc'))
The draws below stay inside these ranges and needn't reach their ends.
Inputs may be any that keep to these rules, and one draw needn't show every extreme that they name: Key positions from valid_count[0] on are padding and take no weight.
All inputs are finite; a program needn't handle non-finite values.
Results may differ from the reference program's by a relative error of at most 0.015.
The reference program's roundings to bfloat16 on the way count: a program that leaves them out, or rounds other values in their place, can miss the bound.
Values may be sent and summed in bfloat16 or wider, within the bound.
A program may use at most 64 MiB of HBM per device.

```python
import math
import jax
import jax.numpy as jnp
from jax import lax

D = 5120
HEAD_DIM = 128
GROUPS = 4
HEADS = 8
FEATURES = 1024
SEQ_LEN = 2560


def joint_draw(key):
    folded = jax.random.fold_in(key, 4111)
    subkeys = jax.random.split(folded, 5)
    column_head = jnp.arange(FEATURES) // HEAD_DIM
    rising = 1.0 + 2.0 * column_head.astype(jnp.float32) / max(HEADS - 1, 1)
    column_scale = rising * jnp.exp(jax.random.uniform(subkeys[0], (FEATURES,), minval=0.0, maxval=jnp.log(3.0)))
    row_query = jnp.exp(jax.random.uniform(subkeys[1], (SEQ_LEN, 1), minval=0.0, maxval=jnp.log(10.0)))
    row_key = jnp.exp(jax.random.uniform(subkeys[2], (SEQ_LEN, 1), minval=0.0, maxval=jnp.log(10.0)))
    query_draw = jax.random.normal(subkeys[3], (SEQ_LEN, FEATURES)) * row_query * column_scale[None, :]
    key_draw = jax.random.normal(subkeys[4], (SEQ_LEN, FEATURES)) * row_key * column_scale[None, :]
    query_draw = jnp.clip(query_draw, -2000.0, 2000.0)
    key_draw = jnp.clip(key_draw, -2000.0, 2000.0)
    return (query_draw.astype(jnp.bfloat16), key_draw.astype(jnp.bfloat16))


def draw_queries(key, part):
    return joint_draw(key)[0]


def draw_keys(key, part):
    return joint_draw(key)[1]


def spiked(drawn, stream_key, source, target, parts, factor):
    owner, partner = [(jnp.arange(drawn.shape[position]) // (drawn.shape[position] // parts)).reshape([-1 if axis == position else 1 for axis in range(drawn.ndim)]) for position in (source, target)]
    chosen = jax.random.permutation(stream_key, parts)[partner]
    strong = (owner == chosen) | (owner == (partner + parts // 2) % parts)
    return jnp.where(strong, factor * drawn, drawn)


def steps_of(key, shape, cuts, smallest, top_value):
    gain, own = 1.0, jax.random.fold_in(key, 6)
    for position, parts in cuts:
        heights = jnp.exp(jax.random.uniform(jax.random.fold_in(own, position), (parts,), jnp.float32, smallest / len(cuts), top_value / len(cuts)))
        gain = gain * jnp.repeat(heights, shape[position] // parts).reshape([-1 if axis == position else 1 for axis in range(len(shape))])
    return gain


def normal_values(stream_key, dims, scale, most, pieces=(), kind=jnp.bfloat16):
    result = scale * jax.random.normal(stream_key, dims, jnp.float32)
    if pieces:
        result = result * steps_of(stream_key, dims, pieces, -0.22, 0.18)
    return jnp.clip(result, -most, most).astype(kind)


def bell_draw_with(stream_key, extent, width, bound, pieces, heavy, kind=jnp.bfloat16):
    drawn = width * jax.random.normal(stream_key, extent, jnp.float32)
    if pieces:
        drawn = drawn * steps_of(stream_key, extent, pieces, -0.22, 0.18)
    return jnp.clip(spiked(drawn, jax.random.fold_in(stream_key, 3), *heavy), -bound, bound).astype(kind)


def setup_inputs(seed: int = 0) -> dict:
    key_list = jax.random.split(jax.random.key(seed), 9)
    queries = draw_queries(jax.random.fold_in(key_list[8], 71), 0)
    keys = draw_keys(jax.random.fold_in(key_list[8], 71), 0)
    values = normal_values(key_list[2], (SEQ_LEN, FEATURES), 1.0, 6.0, ((0, 8), (1, 4)))
    out_weight = bell_draw_with(key_list[3], (FEATURES, D), FEATURES ** -0.5, 0.25, ((0, 4), (1, 8)), (0, 1, 8, 2.0))
    q_gain = jnp.clip(jnp.exp(math.log(3.0) - 1.3862944 * jax.random.uniform(key_list[4], (FEATURES,), jnp.float32) ** steps_of(key_list[4], (FEATURES,), ((0, 4),), -0.2, 0.2)), 0.75, 3.0)
    k_gain = jnp.clip(jnp.exp(math.log(3.0) - 1.3862944 * jax.random.uniform(key_list[5], (FEATURES,), jnp.float32) ** steps_of(key_list[5], (FEATURES,), ((0, 4),), -0.2, 0.2)), 0.75, 3.0)
    gate = jnp.clip(jnp.exp(math.log(8.0) - 2.0794415 * jax.random.uniform(key_list[6], (D,), jnp.float32) ** steps_of(key_list[6], (D,), ((0, 4),), -0.2, 0.2)), 1.0, 8.0)
    valid_count = jax.random.randint(key_list[7], (1,), SEQ_LEN // 2, SEQ_LEN + 1).astype(jnp.int32)
    return {"queries": queries, "keys": keys, "values": values, "out_weight": out_weight, "q_gain": q_gain, "k_gain": k_gain, "gate": gate, "valid_count": valid_count}


epsilon = 1e-06

def normalize(matrix, gain_row):
    values32 = matrix.astype(jnp.float32)
    mean_square = lax.optimization_barrier(jnp.mean(values32 * values32, axis=1, keepdims=True))
    return (values32 * lax.rsqrt(mean_square + epsilon) * gain_row[None, :]).astype(jnp.bfloat16)

def reference(queries, keys, values, out_weight, q_gain, k_gain, gate, valid_count):
    query_norm = normalize(queries, q_gain)
    key_norm = normalize(keys, k_gain)
    key_limit = valid_count[0]
    usable = jnp.arange(SEQ_LEN, dtype=jnp.int32) < key_limit
    score_scale = HEAD_DIM ** (-0.5)
    block_size = 512 if SEQ_LEN % 512 == 0 else SEQ_LEN

    def split_heads(matrix):
        return matrix.reshape(SEQ_LEN, HEADS, HEAD_DIM).transpose(1, 0, 2)

    def attend_head(triple):
        query_head, key_head, value_head = triple
        query_blocks = query_head.reshape(SEQ_LEN // block_size, block_size, HEAD_DIM)

        def attend_block(query_block):
            scores = jnp.dot(query_block, jnp.transpose(key_head), preferred_element_type=jnp.float32) * score_scale
            scores = jnp.where(usable[None, :], scores, -jnp.inf)
            row_max = lax.optimization_barrier(jnp.max(scores, axis=1, keepdims=True))
            weights = jnp.exp(scores - row_max)
            numerator = jnp.dot(weights.astype(jnp.bfloat16), value_head, preferred_element_type=jnp.float32)
            return numerator / lax.optimization_barrier(jnp.sum(weights, axis=1, keepdims=True))
        return lax.map(attend_block, query_blocks).reshape(SEQ_LEN, HEAD_DIM)
    head_outputs = lax.map(attend_head, (split_heads(query_norm), split_heads(key_norm), split_heads(values)))
    attended = head_outputs.transpose(1, 0, 2).reshape(SEQ_LEN, FEATURES).astype(jnp.bfloat16)
    group_width = FEATURES // GROUPS
    attended_groups = attended.reshape(SEQ_LEN, GROUPS, group_width).transpose(1, 0, 2)
    weight_groups = out_weight.reshape(GROUPS, group_width, D)

    def add_group(running, pair):
        group_rows, group_weight = pair
        partial_sum = jnp.dot(group_rows, group_weight, preferred_element_type=jnp.float32).astype(jnp.bfloat16)
        partial_sum = lax.optimization_barrier(partial_sum)
        return (running + partial_sum.astype(jnp.float32), None)
    projected, _ = lax.scan(add_group, jnp.zeros((SEQ_LEN, D), jnp.float32), (attended_groups, weight_groups))
    return (gate[None, :] * projected).astype(jnp.bfloat16)
```

```python
import jax
import jax.numpy as jnp
from jax import lax
from jax.experimental import pallas as pl
from jax.experimental.pallas import tpu as pltpu
from jax.sharding import PartitionSpec as P

HEAD_DIM = 128


epsilon = 1e-06
lowest_score = -1e30


def normalize(matrix, squares, gain_row, feature_count):
    inverse_rms = lax.rsqrt(squares / feature_count + epsilon)
    return (matrix.astype(jnp.float32) * inverse_rms[:, None] * gain_row[None, :]).astype(
        jnp.bfloat16
    )


def absorb(carried, query_heads, key_block, value_block, offset, key_limit):
    running_sum, running_max, running_mass = carried
    scale_factor = query_heads.shape[2] ** (-0.5)
    scores = (
        jnp.einsum("qhd,khd->hqk", query_heads, key_block, preferred_element_type=jnp.float32)
        * scale_factor
    )
    position = offset + jnp.arange(key_block.shape[0], dtype=jnp.int32)
    usable = (position < key_limit)[None, None, :]
    masked = jnp.where(usable, scores, lowest_score)
    new_max = jnp.maximum(running_max, jnp.max(masked, axis=2))
    weights = jnp.where(usable, jnp.exp(masked - new_max[:, :, None]), 0.0)
    factor = jnp.exp(running_max - new_max)
    running_mass = running_mass * factor + jnp.sum(weights, axis=2)
    running_sum = running_sum * factor[:, :, None] + jnp.einsum(
        "hqk,khd->hqd",
        weights.astype(jnp.bfloat16),
        value_block,
        preferred_element_type=jnp.float32,
    )
    return (running_sum, new_max, running_mass)


def absorb_blocks(carried, query_heads, key_rows, value_rows, key_limit):
    row_total = key_rows.shape[0]
    block_size = 512
    block_count = row_total // block_size
    key_blocks = key_rows.reshape((block_count, block_size) + key_rows.shape[1:])
    value_blocks = value_rows.reshape((block_count, block_size) + value_rows.shape[1:])

    def absorb_block(running, triple):
        block_number, key_block, value_block = triple
        return (
            absorb(
                running, query_heads, key_block, value_block, block_number * block_size, key_limit
            ),
            None,
        )

    numbers = jnp.arange(block_count, dtype=jnp.int32)
    carried, _ = lax.scan(absorb_block, carried, (numbers, key_blocks, value_blocks))
    return carried


def visit(carried, query_heads, key_rows, value_rows, offset, key_limit):
    return lax.cond(
        offset < key_limit,
        lambda running: absorb_blocks(running, query_heads, key_rows, value_rows, key_limit),
        lambda running: running,
        carried,
    )


def local(queries, keys, values, out_weight, q_gain, k_gain, gate, valid_count):
    row_count = queries.shape[0]
    local_heads = queries.shape[1] // HEAD_DIM
    feature_count = queries.shape[1] * lax.axis_size(("head", "enc"))
    key_limit = valid_count[0]
    query_squares = jnp.sum(jnp.square(queries.astype(jnp.float32)), axis=1)
    key_squares = jnp.sum(jnp.square(keys.astype(jnp.float32)), axis=1)
    query_totals, key_totals = lax.psum((query_squares, key_squares), ("head", "enc"))
    query_heads = normalize(queries, query_totals, q_gain, feature_count).reshape(
        row_count, local_heads, HEAD_DIM
    )
    key_heads = normalize(keys, key_totals, k_gain, feature_count).reshape(
        row_count, local_heads, HEAD_DIM
    )
    value_heads = values.reshape(row_count, local_heads, HEAD_DIM)
    initial = (
        jnp.zeros((local_heads, row_count, HEAD_DIM), jnp.float32),
        jnp.full((local_heads, row_count), lowest_score, jnp.float32),
        jnp.zeros((local_heads, row_count), jnp.float32),
    )
    running_sum, running_max, running_mass = visit(
        initial,
        query_heads,
        lax.all_gather(key_heads, "seq", axis=0, tiled=True),
        lax.all_gather(value_heads, "seq", axis=0, tiled=True),
        jnp.int32(0),
        key_limit,
    )
    attended = (running_sum / running_mass[:, :, None]).transpose(1, 0, 2)
    attended = attended.reshape(row_count, local_heads * HEAD_DIM).astype(jnp.bfloat16)
    terms = jnp.dot(
        attended,
        lax.all_gather(out_weight, "seq", axis=1, tiled=True),
        preferred_element_type=jnp.float32,
    )
    summed = lax.psum_scatter(
        terms.astype(jnp.bfloat16), ("head", "enc"), scatter_dimension=1, tiled=True
    ).astype(jnp.float32)
    return (gate[None, :] * summed).astype(jnp.bfloat16)


def fused_kernel(
    limit_ref, q_ref, k_ref, v_ref, w_ref, qg_ref, kg_ref, gate_ref, out_ref,
    sums, kv_send, kv_all, q_send, q_both, w_line, w_all, att_send, att_all,
    sums_ss, sums_rs, mir_ss, mir_rs, kv_ss, kv_rs, wl_ss, wl_rs, w2_ss, w2_rs,
    am_ss, a_ss, a_rs,
):
    seq_size = lax.axis_size("seq")
    enc_size = lax.axis_size("enc")
    groups = lax.axis_size("head") * enc_size
    rows = q_ref.shape[0]
    half = seq_size // 2
    inner = seq_size // groups
    outer = seq_size // inner
    outer_half = outer // 2
    feature_count = q_ref.shape[1] * groups
    s = lax.axis_index("seq")
    g = lax.axis_index("head") * enc_size + lax.axis_index("enc")
    head = s // half
    place = s % half
    mirror = (s + half) % seq_size
    a, b = s // inner, s % inner
    a_mirror = (a + outer_half) % outer
    a_base = (a // outer_half) * outer_half

    def where_is(seq_index, group):
        return (seq_index, group // enc_size, group % enc_size)

    def send(src, dst, send_sem, recv_sem, seq_index, group):
        pltpu.make_async_remote_copy(
            src_ref=src, dst_ref=dst, send_sem=send_sem, recv_sem=recv_sem,
            device_id=where_is(seq_index, group), device_id_type=pl.DeviceIdType.MESH,
        ).start()

    def wait(ref, sem):
        pltpu.make_async_copy(ref, ref, sem).wait()

    def group_peer(r):
        return (g + r) % groups

    def half_peer(r):
        return head * half + (place + r) % half

    def line_peer(r):
        return a_base + (a - a_base + r) % outer_half

    barrier = pltpu.get_barrier_semaphore()
    peers = []
    for rb in range(inner):
        for r in range(groups):
            if rb or r:
                peers.append((a * inner + (b + rb) % inner, group_peer(r)))
    for ra in range(outer_half):
        for rb in range(inner):
            if ra:
                peers.append((line_peer(ra) * inner + (b + rb) % inner, g))
    peers.append((mirror, g))
    for peer in peers:
        pl.semaphore_signal(
            barrier, inc=1, device_id=where_is(*peer), device_id_type=pl.DeviceIdType.MESH
        )
    pl.semaphore_wait(barrier, len(peers))

    def spread_piece(src, slot, x):
        for rb in range(inner):
            target = a * inner + (b + rb) % inner
            if rb == 0:
                @pl.when(x == g)
                def _():
                    pltpu.make_async_copy(src, w_all.at[b, g], w2_rs.at[b, g]).start()

                @pl.when(x != g)
                def _():
                    send(src, w_all.at[b, g], w2_ss.at[slot, rb], w2_rs.at[b, g], target, x)
            else:
                send(src, w_all.at[b, g], w2_ss.at[slot, rb], w2_rs.at[b, g], target, x)

    spread_piece(w_ref, 0, a)

    ones = jnp.ones((8, q_ref.shape[1]), jnp.float32)

    def row_sums(ref):
        value = ref[...].astype(jnp.float32)
        return lax.dot_general(
            ones, value * value, (((1,), (1,)), ((), ())),
            precision=lax.Precision.HIGHEST, preferred_element_type=jnp.float32,
        )

    sums[g, 0:8, :] = row_sums(q_ref)
    sums[g, 8:16, :] = row_sums(k_ref)
    for r in range(1, groups):
        send(sums.at[g], sums.at[g], sums_ss.at[r], sums_rs.at[g], s, group_peer(r))
    for r in range(1, groups):
        wait(sums.at[group_peer(r)], sums_rs.at[group_peer(r)])
    total = sums[0]
    for r in range(1, groups):
        total = total + sums[r]
    eighth = jnp.full((8, HEAD_DIM), 0.125, jnp.float32)

    def inverse(row_block):
        column = lax.dot_general(
            row_block, eighth, (((0,), (0,)), ((), ())),
            precision=lax.Precision.HIGHEST, preferred_element_type=jnp.float32,
        )
        return lax.rsqrt(column / feature_count + epsilon)

    q_inverse = inverse(total[0:8])
    k_inverse = inverse(total[8:16])

    def normed(ref, factor, gain, which):
        columns = pl.ds(pl.multiple_of(which * HEAD_DIM, HEAD_DIM), HEAD_DIM)
        return (ref[:, columns].astype(jnp.float32) * factor * gain[:, columns]).astype(
            jnp.bfloat16
        )

    def plain(ref, which):
        return ref[:, pl.ds(pl.multiple_of(which * HEAD_DIM, HEAD_DIM), HEAD_DIM)]

    kv_send[0] = normed(k_ref, k_inverse, kg_ref, 1 - head)
    kv_send[1] = plain(v_ref, 1 - head)
    send(kv_send, kv_all.at[s], mir_ss.at[0], kv_rs.at[s], mirror, g)
    q_send[...] = normed(q_ref, q_inverse, qg_ref, 1 - head)
    send(q_send, q_both.at[0], mir_ss.at[1], mir_rs, mirror, g)
    kv_all[s, 0] = normed(k_ref, k_inverse, kg_ref, head)
    kv_all[s, 1] = plain(v_ref, head)
    for r in range(1, half):
        send(kv_all.at[s], kv_all.at[s], kv_ss.at[0, r], kv_rs.at[s], half_peer(r), g)
    send(w_ref, w_line.at[a], wl_ss.at[0, 0], wl_rs.at[a], mirror, g)
    for r in range(1, outer_half):
        send(w_ref, w_line.at[a], wl_ss.at[0, r], wl_rs.at[a], line_peer(r) * inner + b, g)
    q_both[1] = normed(q_ref, q_inverse, qg_ref, head)

    wait(kv_all.at[mirror], kv_rs.at[mirror])
    for r in range(1, half):
        send(
            kv_all.at[mirror], kv_all.at[mirror], kv_ss.at[1, r], kv_rs.at[mirror],
            half_peer(r), g,
        )
    for r in range(1, outer_half):
        x = line_peer(r)
        wait(w_line.at[x], wl_rs.at[x])
        spread_piece(w_line.at[x], 1 + r, x)
    wait(w_line.at[a_mirror], wl_rs.at[a_mirror])
    for r in range(1, outer_half):
        send(
            w_line.at[a_mirror], w_line.at[a_mirror], wl_ss.at[1, r], wl_rs.at[a_mirror],
            line_peer(r) * inner + b, g,
        )
    spread_piece(w_line.at[a_mirror], 1, a_mirror)

    for r in range(1, half):
        for block in (half_peer(r), (half_peer(r) + half) % seq_size):
            wait(kv_all.at[block], kv_rs.at[block])
    wait(q_both.at[0], mir_rs)

    limit = limit_ref[0]
    scale_factor = HEAD_DIM ** (-0.5)
    key_count = seq_size * rows

    def attend(query):
        keys_flat = kv_all[:, 0].reshape(key_count, HEAD_DIM)
        values_flat = kv_all[:, 1].reshape(key_count, HEAD_DIM)
        scores = lax.dot_general(
            query, keys_flat, (((1,), (1,)), ((), ())), preferred_element_type=jnp.float32
        ) * scale_factor
        position = lax.broadcasted_iota(jnp.int32, scores.shape, 1)
        masked = jnp.where(position < limit, scores, lowest_score)
        weights = jnp.exp(masked - jnp.max(masked, axis=1, keepdims=True))
        mass = jnp.sum(weights, axis=1, keepdims=True)
        mixed = jnp.dot(
            weights.astype(jnp.bfloat16), values_flat, preferred_element_type=jnp.float32
        )
        return (mixed / mass).astype(jnp.bfloat16)

    att_send[...] = attend(q_both[0])
    send(att_send, att_all.at[g, head], am_ss, a_rs.at[g, head], mirror, g)
    for r in range(1, outer_half):
        x = (line_peer(r) + outer_half) % outer
        wait(w_line.at[x], wl_rs.at[x])
        spread_piece(w_line.at[x], outer_half + r, x)
    att_all[g, head] = attend(q_both[1])
    for r in range(1, groups):
        send(
            att_all.at[g, head], att_all.at[g, head], a_ss.at[0, r], a_rs.at[g, head],
            s, group_peer(r),
        )
    other = 1 - head
    wait(att_all.at[g, other], a_rs.at[g, other])
    for r in range(1, groups):
        send(
            att_all.at[g, other], att_all.at[g, other], a_ss.at[1, r], a_rs.at[g, other],
            s, group_peer(r),
        )
    for r in range(1, groups):
        for which in range(2):
            wait(att_all.at[group_peer(r), which], a_rs.at[group_peer(r), which])

    width = w_ref.shape[1]
    for piece in range(inner):
        summed = None
        for group in range(groups):
            wait(w_all.at[piece, group], w2_rs.at[piece, group])
            lhs = jnp.concatenate([att_all[group, 0], att_all[group, 1]], axis=1)
            term = jnp.dot(lhs, w_all[piece, group], preferred_element_type=jnp.float32)
            term = term.astype(jnp.bfloat16).astype(jnp.float32)
            summed = term if summed is None else summed + term
        columns = slice(piece * width, (piece + 1) * width)
        out_ref[:, columns] = (gate_ref[:, columns] * summed).astype(jnp.bfloat16)

    for r in range(1, groups):
        wait(sums.at[g], sums_ss.at[r])
    wait(kv_send, mir_ss.at[0])
    wait(q_send, mir_ss.at[1])
    for turn in range(2):
        for r in range(1, half):
            wait(kv_all.at[s], kv_ss.at[turn, r])
        for r in range(1, outer_half):
            wait(w_ref, wl_ss.at[turn, r])
        for r in range(1, groups):
            wait(att_send, a_ss.at[turn, r])
    wait(w_ref, wl_ss.at[0, 0])
    wait(att_send, am_ss)
    pieces = [(0, a), (1, a_mirror)]
    for r in range(1, outer_half):
        pieces.append((1 + r, line_peer(r)))
        pieces.append((outer_half + r, (line_peer(r) + outer_half) % outer))
    for slot, x in pieces:
        for rb in range(inner):
            if rb == 0:
                @pl.when(x != g)
                def _():
                    wait(w_ref, w2_ss.at[slot, rb])
            else:
                wait(w_ref, w2_ss.at[slot, rb])


def fused(queries, keys, values, out_weight, q_gain, k_gain, gate, valid_count):
    seq_size = lax.axis_size("seq")
    groups = lax.axis_size("head") * lax.axis_size("enc")
    inner = seq_size // groups
    outer = seq_size // inner
    rows, local_width = queries.shape
    depth, width = out_weight.shape
    half = seq_size // 2
    outer_half = outer // 2
    bf16, f32 = jnp.bfloat16, jnp.float32
    dma = pltpu.SemaphoreType.DMA
    vmem = pl.BlockSpec(memory_space=pltpu.VMEM)
    return pl.pallas_call(
        fused_kernel,
        out_shape=jax.ShapeDtypeStruct((rows, width * inner), bf16),
        in_specs=[pl.BlockSpec(memory_space=pltpu.SMEM)] + [vmem] * 7,
        out_specs=vmem,
        scratch_shapes=[
            pltpu.VMEM((groups, 16, rows), f32),
            pltpu.VMEM((2, rows, HEAD_DIM), bf16),
            pltpu.VMEM((seq_size, 2, rows, HEAD_DIM), bf16),
            pltpu.VMEM((rows, HEAD_DIM), bf16),
            pltpu.VMEM((2, rows, HEAD_DIM), bf16),
            pltpu.VMEM((outer, depth, width), bf16),
            pltpu.VMEM((inner, groups, depth, width), bf16),
            pltpu.VMEM((rows, HEAD_DIM), bf16),
            pltpu.VMEM((groups, 2, rows, HEAD_DIM), bf16),
            dma((groups,)), dma((groups,)),
            dma((2,)), dma,
            dma((2, half)), dma((seq_size,)),
            dma((2, outer_half)), dma((outer,)),
            dma((outer, inner)), dma((inner, groups)),
            dma, dma((2, groups)), dma((groups, 2)),
        ],
        compiler_params=pltpu.CompilerParams(
            collective_id=0, has_side_effects=True, vmem_limit_bytes=56 * 2**20
        ),
    )(
        valid_count, queries, keys, values, out_weight,
        q_gain[None, :], k_gain[None, :], gate[None, :],
    )


def one_kernel_fits(mesh, queries, out_weight):
    sizes = mesh.shape
    seq_size, groups = sizes["seq"], sizes["head"] * sizes["enc"]
    return (
        seq_size % groups == 0
        and groups % 2 == 0
        and queries.shape[1] == 2 * groups * HEAD_DIM
        and (out_weight.shape[1] // seq_size) % HEAD_DIM == 0
    )


def solution(mesh):
    placed = (
        P("seq", ("head", "enc")),
        P("seq", ("head", "enc")),
        P("seq", ("head", "enc")),
        P(("head", "enc"), "seq"),
        P(("head", "enc")),
        P(("head", "enc")),
        P(("head", "enc")),
        P(),
    )

    def run(*arguments):
        body = fused if one_kernel_fits(mesh, arguments[0], arguments[3]) else local
        return jax.shard_map(
            body, mesh=mesh, in_specs=placed, out_specs=P("seq", ("head", "enc")),
            check_vma=False,
        )(*arguments)

    return run
```

```python
import jax
import jax.numpy as jnp
from jax import lax
from jax.experimental import pallas as pl
from jax.experimental.pallas import tpu as pltpu
from jax.sharding import PartitionSpec as P

HEAD_DIM = 128


epsilon = 1e-06
lowest_score = -1e30


def normalize(matrix, squares, gain_row, feature_count):
    inverse_rms = lax.rsqrt(squares / feature_count + epsilon)
    return (matrix.astype(jnp.float32) * inverse_rms[:, None] * gain_row[None, :]).astype(
        jnp.bfloat16
    )


def absorb(carried, query_heads, key_block, value_block, offset, key_limit):
    running_sum, running_max, running_mass = carried
    scale_factor = query_heads.shape[2] ** (-0.5)
    scores = (
        jnp.einsum("qhd,khd->hqk", query_heads, key_block, preferred_element_type=jnp.float32)
        * scale_factor
    )
    position = offset + jnp.arange(key_block.shape[0], dtype=jnp.int32)
    usable = (position < key_limit)[None, None, :]
    masked = jnp.where(usable, scores, lowest_score)
    new_max = jnp.maximum(running_max, jnp.max(masked, axis=2))
    weights = jnp.where(usable, jnp.exp(masked - new_max[:, :, None]), 0.0)
    factor = jnp.exp(running_max - new_max)
    running_mass = running_mass * factor + jnp.sum(weights, axis=2)
    running_sum = running_sum * factor[:, :, None] + jnp.einsum(
        "hqk,khd->hqd",
        weights.astype(jnp.bfloat16),
        value_block,
        preferred_element_type=jnp.float32,
    )
    return (running_sum, new_max, running_mass)


def absorb_blocks(carried, query_heads, key_rows, value_rows, key_limit):
    row_total = key_rows.shape[0]
    block_size = 512
    block_count = row_total // block_size
    key_blocks = key_rows.reshape((block_count, block_size) + key_rows.shape[1:])
    value_blocks = value_rows.reshape((block_count, block_size) + value_rows.shape[1:])

    def absorb_block(running, triple):
        block_number, key_block, value_block = triple
        return (
            absorb(
                running, query_heads, key_block, value_block, block_number * block_size, key_limit
            ),
            None,
        )

    numbers = jnp.arange(block_count, dtype=jnp.int32)
    carried, _ = lax.scan(absorb_block, carried, (numbers, key_blocks, value_blocks))
    return carried


def visit(carried, query_heads, key_rows, value_rows, offset, key_limit):
    return lax.cond(
        offset < key_limit,
        lambda running: absorb_blocks(running, query_heads, key_rows, value_rows, key_limit),
        lambda running: running,
        carried,
    )


def local(queries, keys, values, out_weight, q_gain, k_gain, gate, valid_count):
    row_count = queries.shape[0]
    local_heads = queries.shape[1] // HEAD_DIM
    feature_count = queries.shape[1] * lax.axis_size(("head", "enc"))
    key_limit = valid_count[0]
    query_squares = jnp.sum(jnp.square(queries.astype(jnp.float32)), axis=1)
    key_squares = jnp.sum(jnp.square(keys.astype(jnp.float32)), axis=1)
    query_totals, key_totals = lax.psum((query_squares, key_squares), ("head", "enc"))
    query_heads = normalize(queries, query_totals, q_gain, feature_count).reshape(
        row_count, local_heads, HEAD_DIM
    )
    key_heads = normalize(keys, key_totals, k_gain, feature_count).reshape(
        row_count, local_heads, HEAD_DIM
    )
    value_heads = values.reshape(row_count, local_heads, HEAD_DIM)
    initial = (
        jnp.zeros((local_heads, row_count, HEAD_DIM), jnp.float32),
        jnp.full((local_heads, row_count), lowest_score, jnp.float32),
        jnp.zeros((local_heads, row_count), jnp.float32),
    )
    running_sum, running_max, running_mass = visit(
        initial,
        query_heads,
        lax.all_gather(key_heads, "seq", axis=0, tiled=True),
        lax.all_gather(value_heads, "seq", axis=0, tiled=True),
        jnp.int32(0),
        key_limit,
    )
    attended = (running_sum / running_mass[:, :, None]).transpose(1, 0, 2)
    attended = attended.reshape(row_count, local_heads * HEAD_DIM).astype(jnp.bfloat16)
    terms = jnp.dot(
        attended,
        lax.all_gather(out_weight, "seq", axis=1, tiled=True),
        preferred_element_type=jnp.float32,
    )
    summed = lax.psum_scatter(
        terms.astype(jnp.bfloat16), ("head", "enc"), scatter_dimension=1, tiled=True
    ).astype(jnp.float32)
    return (gate[None, :] * summed).astype(jnp.bfloat16)


def fused_kernel(
    limit_ref, q_ref, k_ref, v_ref, w_ref, qg_ref, kg_ref, gate_ref, out_ref,
    sums, kv_send, kv_all, q_send, q_all, w_line, w_all, att_send, att_all,
    sums_ss, sums_rs, kv1_ss, q1_ss, q_rs, kv2_ss, kv3_ss, kv_rs, wl_ss, wl_rs, w2_ss, w2_rs,
    a1_ss, a2_ss, a_rs,
):
    seq_size = lax.axis_size("seq")
    enc_size = lax.axis_size("enc")
    groups = lax.axis_size("head") * enc_size
    rows = q_ref.shape[0]
    inner = seq_size // groups
    outer = seq_size // inner
    outer_half = outer // 2
    shares = outer // enc_size
    feature_count = q_ref.shape[1] * groups
    s = lax.axis_index("seq")
    e = lax.axis_index("enc")
    h = lax.axis_index("head")
    g = h * enc_size + e
    a, b = s // inner, s % inner
    a_mirror = (a + outer_half) % outer
    mirror = a_mirror * inner + b
    a_base = (a // outer_half) * outer_half

    def where_is(seq_index, group):
        return (seq_index, group // enc_size, group % enc_size)

    def send(src, dst, send_sem, recv_sem, seq_index, group):
        pltpu.make_async_remote_copy(
            src_ref=src, dst_ref=dst, send_sem=send_sem, recv_sem=recv_sem,
            device_id=where_is(seq_index, group), device_id_type=pl.DeviceIdType.MESH,
        ).start()

    def wait(ref, sem):
        pltpu.make_async_copy(ref, ref, sem).wait()

    def group_peer(r):
        return (g + r) % groups

    def line_peer(r):
        return a_base + (a - a_base + r) % outer_half

    barrier = pltpu.get_barrier_semaphore()
    peers = []
    for rb in range(inner):
        for r in range(groups):
            if rb or r:
                peers.append((a * inner + (b + rb) % inner, group_peer(r)))
    for ra in range(1, outer):
        for re in range(enc_size):
            peers.append((((a + ra) % outer) * inner + b, h * enc_size + re))
    for peer in peers:
        pl.semaphore_signal(
            barrier, inc=1, device_id=where_is(*peer), device_id_type=pl.DeviceIdType.MESH
        )
    pl.semaphore_wait(barrier, len(peers))

    def spread_piece(src, slot, x):
        for rb in range(inner):
            target = a * inner + (b + rb) % inner
            if rb == 0:
                @pl.when(x == g)
                def _():
                    pltpu.make_async_copy(src, w_all.at[b, g], w2_rs.at[b, g]).start()

                @pl.when(x != g)
                def _():
                    send(src, w_all.at[b, g], w2_ss.at[slot, rb], w2_rs.at[b, g], target, x)
            else:
                send(src, w_all.at[b, g], w2_ss.at[slot, rb], w2_rs.at[b, g], target, x)

    ones = jnp.ones((8, q_ref.shape[1]), jnp.float32)

    def row_sums(ref):
        value = ref[...].astype(jnp.float32)
        return lax.dot_general(
            ones, value * value, (((1,), (1,)), ((), ())),
            precision=lax.Precision.HIGHEST, preferred_element_type=jnp.float32,
        )

    sums[g, 0:8, :] = row_sums(q_ref)
    sums[g, 8:16, :] = row_sums(k_ref)
    for r in range(1, groups):
        send(sums.at[g], sums.at[g], sums_ss.at[r], sums_rs.at[g], s, group_peer(r))
    for r in range(1, outer_half):
        send(w_ref, w_line.at[a], wl_ss.at[0, r], wl_rs.at[a], line_peer(r) * inner + b, g)
    send(w_ref, w_line.at[a], wl_ss.at[0, 0], wl_rs.at[a], mirror, g)
    spread_piece(w_ref, 0, a)

    for r in range(1, groups):
        wait(sums.at[group_peer(r)], sums_rs.at[group_peer(r)])
    total = sums[0]
    for r in range(1, groups):
        total = total + sums[r]
    eighth = jnp.full((8, HEAD_DIM), 0.125, jnp.float32)

    def inverse(row_block):
        column = lax.dot_general(
            row_block, eighth, (((0,), (0,)), ((), ())),
            precision=lax.Precision.HIGHEST, preferred_element_type=jnp.float32,
        )
        return lax.rsqrt(column / feature_count + epsilon)

    q_inverse = inverse(total[0:8])
    k_inverse = inverse(total[8:16])

    def normed(ref, factor, gain, which):
        columns = pl.ds(pl.multiple_of(which * HEAD_DIM, HEAD_DIM), HEAD_DIM)
        return (ref[:, columns].astype(jnp.float32) * factor * gain[:, columns]).astype(
            jnp.bfloat16
        )

    def plain(ref, which):
        return ref[:, pl.ds(pl.multiple_of(which * HEAD_DIM, HEAD_DIM), HEAD_DIM)]

    catcher = a % enc_size
    for i in range(2):
        plane = e * 2 + i
        local_turn = jnp.logical_and(plane == a, catcher == e)
        target = plane * inner + b
        target_group = h * enc_size + catcher
        kv_send[i, 0] = normed(k_ref, k_inverse, kg_ref, i)
        kv_send[i, 1] = plain(v_ref, i)
        q_send[i] = normed(q_ref, q_inverse, qg_ref, i)

        @pl.when(local_turn)
        def _():
            pltpu.make_async_copy(kv_send.at[i], kv_all.at[s], kv_rs.at[s]).start()
            pltpu.make_async_copy(
                q_send.at[i], q_all.at[a // enc_size], q_rs.at[a // enc_size]
            ).start()

        @pl.when(jnp.logical_not(local_turn))
        def _():
            send(
                kv_send.at[i], kv_all.at[s], kv1_ss.at[i], kv_rs.at[s], target, target_group
            )
            send(
                q_send.at[i], q_all.at[a // enc_size], q1_ss.at[i], q_rs.at[a // enc_size],
                target, target_group,
            )

    for r in range(1, outer_half):
        x = line_peer(r)
        wait(w_line.at[x], wl_rs.at[x])
        spread_piece(w_line.at[x], 1 + r, x)

    def share_of(turn):
        return (a // enc_size + turn) % shares

    def block_at(turn, core, column):
        return (share_of(turn) * enc_size + core) * inner + column

    def pass_on(turn):
        block = block_at(turn, e, b)
        wait(kv_all.at[block], kv_rs.at[block])
        for rb in range(1, inner):
            send(
                kv_all.at[block], kv_all.at[block], kv2_ss.at[turn, enc_size + rb],
                kv_rs.at[block], a * inner + (b + rb) % inner, g,
            )
        for re in range(1, enc_size):
            send(
                kv_all.at[block], kv_all.at[block], kv2_ss.at[turn, re], kv_rs.at[block],
                s, h * enc_size + (e + re) % enc_size,
            )

    def pass_across(turn):
        for rb in range(1, inner):
            block = block_at(turn, e, (b + rb) % inner)
            wait(kv_all.at[block], kv_rs.at[block])
            for re in range(1, enc_size):
                send(
                    kv_all.at[block], kv_all.at[block], kv3_ss.at[turn, rb, re],
                    kv_rs.at[block], s, h * enc_size + (e + re) % enc_size,
                )

    for turn in range(shares):
        pass_on(turn)
    wait(w_line.at[a_mirror], wl_rs.at[a_mirror])
    for r in range(1, outer_half):
        send(
            w_line.at[a_mirror], w_line.at[a_mirror], wl_ss.at[1, r], wl_rs.at[a_mirror],
            line_peer(r) * inner + b, g,
        )
    spread_piece(w_line.at[a_mirror], 1, a_mirror)
    for turn in range(shares):
        pass_across(turn)
    for turn in range(shares):
        for re in range(1, enc_size):
            for rb in range(inner):
                block = block_at(turn, (e + re) % enc_size, (b + rb) % inner)
                wait(kv_all.at[block], kv_rs.at[block])
    for share in range(shares):
        wait(q_all.at[share], q_rs.at[share])

    limit = limit_ref[0]
    scale_factor = HEAD_DIM ** (-0.5)
    key_count = seq_size * rows

    def attend(query):
        keys_flat = kv_all[:, 0].reshape(key_count, HEAD_DIM)
        values_flat = kv_all[:, 1].reshape(key_count, HEAD_DIM)
        scores = lax.dot_general(
            query, keys_flat, (((1,), (1,)), ((), ())), preferred_element_type=jnp.float32
        ) * scale_factor
        position = lax.broadcasted_iota(jnp.int32, scores.shape, 1)
        masked = jnp.where(position < limit, scores, lowest_score)
        weights = jnp.exp(masked - jnp.max(masked, axis=1, keepdims=True))
        mass = jnp.sum(weights, axis=1, keepdims=True)
        mixed = jnp.dot(
            weights.astype(jnp.bfloat16), values_flat, preferred_element_type=jnp.float32
        )
        return (mixed / mass).astype(jnp.bfloat16)

    mine = h * enc_size + a // 2
    which = a % 2
    for turn in range(shares):
        share = share_of(turn + 1)
        plane = share * enc_size + e
        att_send[turn] = attend(q_all[share])

        @pl.when(plane == a)
        def _():
            pltpu.make_async_copy(
                att_send.at[turn], att_all.at[mine, which], a_rs.at[mine, which]
            ).start()

        @pl.when(plane != a)
        def _():
            send(
                att_send.at[turn], att_all.at[mine, which], a1_ss.at[turn],
                a_rs.at[mine, which], plane * inner + b, g,
            )

        if turn == 0:
            for r in range(1, outer_half):
                x = (line_peer(r) + outer_half) % outer
                wait(w_line.at[x], wl_rs.at[x])
                spread_piece(w_line.at[x], outer_half + r, x)

    @pl.when(e == catcher)
    def _():
        for ra in range(outer):
            plane = (a + ra) % outer
            group, i = h * enc_size + plane // 2, plane % 2
            wait(att_all.at[group, i], a_rs.at[group, i])
            for r in range(1, groups):
                send(
                    att_all.at[group, i], att_all.at[group, i], a2_ss.at[ra, r],
                    a_rs.at[group, i], s, group_peer(r),
                )
        for rh in range(enc_size, groups):
            group = (h * enc_size + rh) % groups
            for i in range(2):
                wait(att_all.at[group, i], a_rs.at[group, i])

    @pl.when(e != catcher)
    def _():
        for group in range(groups):
            for i in range(2):
                wait(att_all.at[group, i], a_rs.at[group, i])

    width = w_ref.shape[1]
    for piece in range(inner):
        summed = None
        for group in range(groups):
            wait(w_all.at[piece, group], w2_rs.at[piece, group])
            lhs = jnp.concatenate([att_all[group, 0], att_all[group, 1]], axis=1)
            term = jnp.dot(lhs, w_all[piece, group], preferred_element_type=jnp.float32)
            term = term.astype(jnp.bfloat16).astype(jnp.float32)
            summed = term if summed is None else summed + term
        columns = slice(piece * width, (piece + 1) * width)
        out_ref[:, columns] = (gate_ref[columns][None, :] * summed).astype(jnp.bfloat16)

    for r in range(1, groups):
        wait(sums.at[g], sums_ss.at[r])
    for i in range(2):
        @pl.when(jnp.logical_not(jnp.logical_and(e * 2 + i == a, catcher == e)))
        def _():
            wait(kv_send.at[i], kv1_ss.at[i])
            wait(q_send.at[i], q1_ss.at[i])
    for turn in range(shares):
        for re in range(1, enc_size):
            wait(kv_send.at[0], kv2_ss.at[turn, re])
        for rb in range(1, inner):
            wait(kv_send.at[0], kv2_ss.at[turn, enc_size + rb])
            for re in range(1, enc_size):
                wait(kv_send.at[0], kv3_ss.at[turn, rb, re])

        @pl.when(share_of(turn + 1) * enc_size + e != a)
        def _():
            wait(att_send.at[turn], a1_ss.at[turn])

    @pl.when(e == catcher)
    def _():
        for ra in range(outer):
            for r in range(1, groups):
                wait(att_send.at[0], a2_ss.at[ra, r])

    for turn in range(2):
        for r in range(1, outer_half):
            wait(w_ref, wl_ss.at[turn, r])
    wait(w_ref, wl_ss.at[0, 0])
    pieces = [(0, a), (1, a_mirror)]
    for r in range(1, outer_half):
        pieces.append((1 + r, line_peer(r)))
        pieces.append((outer_half + r, (line_peer(r) + outer_half) % outer))
    for slot, x in pieces:
        for rb in range(inner):
            if rb == 0:
                @pl.when(x != g)
                def _():
                    wait(w_ref, w2_ss.at[slot, rb])
            else:
                wait(w_ref, w2_ss.at[slot, rb])


def fused(queries, keys, values, out_weight, q_gain, k_gain, gate, valid_count):
    seq_size = lax.axis_size("seq")
    groups = lax.axis_size("head") * lax.axis_size("enc")
    inner = seq_size // groups
    outer = seq_size // inner
    rows, local_width = queries.shape
    depth, width = out_weight.shape
    enc_size = lax.axis_size("enc")
    shares = outer // enc_size
    outer_half = outer // 2
    bf16, f32 = jnp.bfloat16, jnp.float32
    dma = pltpu.SemaphoreType.DMA
    vmem = pl.BlockSpec(memory_space=pltpu.VMEM)
    return pl.pallas_call(
        fused_kernel,
        out_shape=jax.ShapeDtypeStruct((rows, width * inner), bf16),
        in_specs=[pl.BlockSpec(memory_space=pltpu.SMEM)] + [vmem] * 7,
        out_specs=vmem,
        scratch_shapes=[
            pltpu.VMEM((groups, 16, rows), f32),
            pltpu.VMEM((2, 2, rows, HEAD_DIM), bf16),
            pltpu.VMEM((seq_size, 2, rows, HEAD_DIM), bf16),
            pltpu.VMEM((2, rows, HEAD_DIM), bf16),
            pltpu.VMEM((shares, rows, HEAD_DIM), bf16),
            pltpu.VMEM((outer, depth, width), bf16),
            pltpu.VMEM((inner, groups, depth, width), bf16),
            pltpu.VMEM((shares, rows, HEAD_DIM), bf16),
            pltpu.VMEM((groups, 2, rows, HEAD_DIM), bf16),
            dma((groups,)), dma((groups,)),
            dma((2,)), dma((2,)), dma((shares,)),
            dma((shares, enc_size + inner)), dma((shares, inner, enc_size)), dma((seq_size,)),
            dma((2, outer_half)), dma((outer,)),
            dma((outer, inner)), dma((inner, groups)),
            dma((shares,)), dma((outer, groups)), dma((groups, 2)),
        ],
        compiler_params=pltpu.CompilerParams(
            collective_id=0, has_side_effects=True, vmem_limit_bytes=56 * 2**20
        ),
    )(
        valid_count, queries, keys, values, out_weight,
        q_gain[None, :], k_gain[None, :], gate,
    )


def one_kernel_fits(mesh, queries, out_weight):
    sizes = mesh.shape
    seq_size, groups = sizes["seq"], sizes["head"] * sizes["enc"]
    return (
        seq_size % groups == 0
        and groups % 2 == 0
        and seq_size // (seq_size // groups) == 2 * sizes["enc"]
        and queries.shape[1] == 2 * groups * HEAD_DIM
        and (out_weight.shape[1] // seq_size) % HEAD_DIM == 0
    )


def solution(mesh):
    placed = (
        P("seq", ("head", "enc")),
        P("seq", ("head", "enc")),
        P("seq", ("head", "enc")),
        P(("head", "enc"), "seq"),
        P(("head", "enc")),
        P(("head", "enc")),
        P(("head", "enc")),
        P(),
    )

    def run(*arguments):
        body = fused if one_kernel_fits(mesh, arguments[0], arguments[3]) else local
        return jax.shard_map(
            body, mesh=mesh, in_specs=placed, out_specs=P("seq", ("head", "enc")),
            check_vma=False,
        )(*arguments)

    return run
```

```python
import jax
import jax.numpy as jnp
from jax import lax
from jax.experimental import pallas as pl
from jax.experimental.pallas import tpu as pltpu
from jax.sharding import PartitionSpec as P

HEAD_DIM = 128


epsilon = 1e-06
lowest_score = -1e30


def normalize(matrix, squares, gain_row, feature_count):
    inverse_rms = lax.rsqrt(squares / feature_count + epsilon)
    return (matrix.astype(jnp.float32) * inverse_rms[:, None] * gain_row[None, :]).astype(
        jnp.bfloat16
    )


def absorb(carried, query_heads, key_block, value_block, offset, key_limit):
    running_sum, running_max, running_mass = carried
    scale_factor = query_heads.shape[2] ** (-0.5)
    scores = (
        jnp.einsum("qhd,khd->hqk", query_heads, key_block, preferred_element_type=jnp.float32)
        * scale_factor
    )
    position = offset + jnp.arange(key_block.shape[0], dtype=jnp.int32)
    usable = (position < key_limit)[None, None, :]
    masked = jnp.where(usable, scores, lowest_score)
    new_max = jnp.maximum(running_max, jnp.max(masked, axis=2))
    weights = jnp.where(usable, jnp.exp(masked - new_max[:, :, None]), 0.0)
    factor = jnp.exp(running_max - new_max)
    running_mass = running_mass * factor + jnp.sum(weights, axis=2)
    running_sum = running_sum * factor[:, :, None] + jnp.einsum(
        "hqk,khd->hqd",
        weights.astype(jnp.bfloat16),
        value_block,
        preferred_element_type=jnp.float32,
    )
    return (running_sum, new_max, running_mass)


def absorb_blocks(carried, query_heads, key_rows, value_rows, key_limit):
    row_total = key_rows.shape[0]
    block_size = 512
    block_count = row_total // block_size
    key_blocks = key_rows.reshape((block_count, block_size) + key_rows.shape[1:])
    value_blocks = value_rows.reshape((block_count, block_size) + value_rows.shape[1:])

    def absorb_block(running, triple):
        block_number, key_block, value_block = triple
        return (
            absorb(
                running, query_heads, key_block, value_block, block_number * block_size, key_limit
            ),
            None,
        )

    numbers = jnp.arange(block_count, dtype=jnp.int32)
    carried, _ = lax.scan(absorb_block, carried, (numbers, key_blocks, value_blocks))
    return carried


def visit(carried, query_heads, key_rows, value_rows, offset, key_limit):
    return lax.cond(
        offset < key_limit,
        lambda running: absorb_blocks(running, query_heads, key_rows, value_rows, key_limit),
        lambda running: running,
        carried,
    )


def local(queries, keys, values, out_weight, q_gain, k_gain, gate, valid_count):
    row_count = queries.shape[0]
    local_heads = queries.shape[1] // HEAD_DIM
    feature_count = queries.shape[1] * lax.axis_size(("head", "enc"))
    key_limit = valid_count[0]
    query_squares = jnp.sum(jnp.square(queries.astype(jnp.float32)), axis=1)
    key_squares = jnp.sum(jnp.square(keys.astype(jnp.float32)), axis=1)
    query_totals, key_totals = lax.psum((query_squares, key_squares), ("head", "enc"))
    query_heads = normalize(queries, query_totals, q_gain, feature_count).reshape(
        row_count, local_heads, HEAD_DIM
    )
    key_heads = normalize(keys, key_totals, k_gain, feature_count).reshape(
        row_count, local_heads, HEAD_DIM
    )
    value_heads = values.reshape(row_count, local_heads, HEAD_DIM)
    initial = (
        jnp.zeros((local_heads, row_count, HEAD_DIM), jnp.float32),
        jnp.full((local_heads, row_count), lowest_score, jnp.float32),
        jnp.zeros((local_heads, row_count), jnp.float32),
    )
    running_sum, running_max, running_mass = visit(
        initial,
        query_heads,
        lax.all_gather(key_heads, "seq", axis=0, tiled=True),
        lax.all_gather(value_heads, "seq", axis=0, tiled=True),
        jnp.int32(0),
        key_limit,
    )
    attended = (running_sum / running_mass[:, :, None]).transpose(1, 0, 2)
    attended = attended.reshape(row_count, local_heads * HEAD_DIM).astype(jnp.bfloat16)
    terms = jnp.dot(
        attended,
        lax.all_gather(out_weight, "seq", axis=1, tiled=True),
        preferred_element_type=jnp.float32,
    )
    summed = lax.psum_scatter(
        terms.astype(jnp.bfloat16), ("head", "enc"), scatter_dimension=1, tiled=True
    ).astype(jnp.float32)
    return (gate[None, :] * summed).astype(jnp.bfloat16)


def fused_kernel(
    limit_ref, q_ref, k_ref, v_ref, w_ref, qg_ref, kg_ref, gate_ref, out_ref,
    sums, kv_send, kv_all, q_send, q_all, w_line, w_all, att_send, att_all,
    sums_ss, sums_rs, kv1_ss, q1_ss, q_rs, kv2_ss, kv3_ss, kv_rs, wl_ss, wl_rs, w2_ss, w2_rs, w3_ss,
    a1_ss, a2_ss, a_rs,
):
    seq_size = lax.axis_size("seq")
    enc_size = lax.axis_size("enc")
    groups = lax.axis_size("head") * enc_size
    rows = q_ref.shape[0]
    inner = seq_size // groups
    outer = seq_size // inner
    outer_half = outer // 2
    shares = outer // enc_size
    feature_count = q_ref.shape[1] * groups
    s = lax.axis_index("seq")
    e = lax.axis_index("enc")
    h = lax.axis_index("head")
    g = h * enc_size + e
    a, b = s // inner, s % inner
    a_mirror = (a + outer_half) % outer
    mirror = a_mirror * inner + b
    a_base = (a // outer_half) * outer_half

    def where_is(seq_index, group):
        return (seq_index, group // enc_size, group % enc_size)

    def send(src, dst, send_sem, recv_sem, seq_index, group):
        pltpu.make_async_remote_copy(
            src_ref=src, dst_ref=dst, send_sem=send_sem, recv_sem=recv_sem,
            device_id=where_is(seq_index, group), device_id_type=pl.DeviceIdType.MESH,
        ).start()

    def wait(ref, sem):
        pltpu.make_async_copy(ref, ref, sem).wait()

    def group_peer(r):
        return (g + r) % groups

    def line_peer(r):
        return a_base + (a - a_base + r) % outer_half

    barrier = pltpu.get_barrier_semaphore()
    peers = []
    for rb in range(inner):
        for r in range(groups):
            if rb or r:
                peers.append((a * inner + (b + rb) % inner, group_peer(r)))
    for ra in range(1, outer):
        for re in range(enc_size):
            peers.append((((a + ra) % outer) * inner + b, h * enc_size + re))
    for peer in peers:
        pl.semaphore_signal(
            barrier, inc=1, device_id=where_is(*peer), device_id_type=pl.DeviceIdType.MESH
        )
    pl.semaphore_wait(barrier, len(peers))

    def by_relay(from_head, from_core, to_head):
        return from_head != to_head

    def relay_pieces():
        for group in range(groups):
            @pl.when(by_relay(group // enc_size, group % enc_size, h))
            def _():
                wait(w_all.at[b, group], w2_rs.at[b, group])
                for rb in range(1, inner):
                    send(
                        w_all.at[b, group], w_all.at[b, group], w3_ss.at[group, rb],
                        w2_rs.at[b, group], a * inner + (b + rb) % inner, g,
                    )

    def spread_piece(src, slot, x):
        for rb in range(inner):
            target = a * inner + (b + rb) % inner
            if rb == 0:
                @pl.when(x == g)
                def _():
                    pltpu.make_async_copy(src, w_all.at[b, g], w2_rs.at[b, g]).start()

                @pl.when(x != g)
                def _():
                    send(src, w_all.at[b, g], w2_ss.at[slot, rb], w2_rs.at[b, g], target, x)
            else:
                @pl.when(jnp.logical_not(by_relay(h, e, x // enc_size)))
                def _():
                    send(src, w_all.at[b, g], w2_ss.at[slot, rb], w2_rs.at[b, g], target, x)

    ones = jnp.ones((8, q_ref.shape[1]), jnp.float32)

    def row_sums(ref):
        value = ref[...].astype(jnp.float32)
        return lax.dot_general(
            ones, value * value, (((1,), (1,)), ((), ())),
            precision=lax.Precision.HIGHEST, preferred_element_type=jnp.float32,
        )

    sums[g, 0:8, :] = row_sums(q_ref)
    sums[g, 8:16, :] = row_sums(k_ref)
    for r in range(1, groups):
        send(sums.at[g], sums.at[g], sums_ss.at[r], sums_rs.at[g], s, group_peer(r))
    for r in range(1, outer_half):
        send(w_ref, w_line.at[a], wl_ss.at[0, r], wl_rs.at[a], line_peer(r) * inner + b, g)
    send(w_ref, w_line.at[a], wl_ss.at[0, 0], wl_rs.at[a], mirror, g)
    spread_piece(w_ref, 0, a)

    for r in range(1, groups):
        wait(sums.at[group_peer(r)], sums_rs.at[group_peer(r)])
    total = sums[0]
    for r in range(1, groups):
        total = total + sums[r]
    eighth = jnp.full((8, HEAD_DIM), 0.125, jnp.float32)

    def inverse(row_block):
        column = lax.dot_general(
            row_block, eighth, (((0,), (0,)), ((), ())),
            precision=lax.Precision.HIGHEST, preferred_element_type=jnp.float32,
        )
        return lax.rsqrt(column / feature_count + epsilon)

    q_inverse = inverse(total[0:8])
    k_inverse = inverse(total[8:16])

    def normed(ref, factor, gain, which):
        columns = pl.ds(pl.multiple_of(which * HEAD_DIM, HEAD_DIM), HEAD_DIM)
        return (ref[:, columns].astype(jnp.float32) * factor * gain[:, columns]).astype(
            jnp.bfloat16
        )

    def plain(ref, which):
        return ref[:, pl.ds(pl.multiple_of(which * HEAD_DIM, HEAD_DIM), HEAD_DIM)]

    catcher = a % enc_size
    for i in range(2):
        plane = e * 2 + i
        local_turn = jnp.logical_and(plane == a, catcher == e)
        target = plane * inner + b
        target_group = h * enc_size + catcher
        kv_send[i, 0] = normed(k_ref, k_inverse, kg_ref, i)
        kv_send[i, 1] = plain(v_ref, i)
        q_send[i] = normed(q_ref, q_inverse, qg_ref, i)

        @pl.when(local_turn)
        def _():
            pltpu.make_async_copy(kv_send.at[i], kv_all.at[s], kv_rs.at[s]).start()
            pltpu.make_async_copy(
                q_send.at[i], q_all.at[a // enc_size], q_rs.at[a // enc_size]
            ).start()

        @pl.when(jnp.logical_not(local_turn))
        def _():
            send(
                kv_send.at[i], kv_all.at[s], kv1_ss.at[i], kv_rs.at[s], target, target_group
            )
            send(
                q_send.at[i], q_all.at[a // enc_size], q1_ss.at[i], q_rs.at[a // enc_size],
                target, target_group,
            )

    for r in range(1, outer_half):
        x = line_peer(r)
        wait(w_line.at[x], wl_rs.at[x])
        spread_piece(w_line.at[x], 1 + r, x)

    def share_of(turn):
        return (a // enc_size + turn) % shares

    def block_at(turn, core, column):
        return (share_of(turn) * enc_size + core) * inner + column

    def pass_on(turn):
        block = block_at(turn, e, b)
        wait(kv_all.at[block], kv_rs.at[block])
        for rb in range(1, inner):
            send(
                kv_all.at[block], kv_all.at[block], kv2_ss.at[turn, enc_size + rb],
                kv_rs.at[block], a * inner + (b + rb) % inner, g,
            )
        for re in range(1, enc_size):
            send(
                kv_all.at[block], kv_all.at[block], kv2_ss.at[turn, re], kv_rs.at[block],
                s, h * enc_size + (e + re) % enc_size,
            )

    def pass_across(turn):
        for rb in range(1, inner):
            block = block_at(turn, e, (b + rb) % inner)
            wait(kv_all.at[block], kv_rs.at[block])
            for re in range(1, enc_size):
                send(
                    kv_all.at[block], kv_all.at[block], kv3_ss.at[turn, rb, re],
                    kv_rs.at[block], s, h * enc_size + (e + re) % enc_size,
                )

    for turn in range(shares):
        pass_on(turn)
    wait(w_line.at[a_mirror], wl_rs.at[a_mirror])
    for r in range(1, outer_half):
        send(
            w_line.at[a_mirror], w_line.at[a_mirror], wl_ss.at[1, r], wl_rs.at[a_mirror],
            line_peer(r) * inner + b, g,
        )
    spread_piece(w_line.at[a_mirror], 1, a_mirror)
    for turn in range(shares):
        pass_across(turn)
    near = g // outer_half == a // outer_half

    @pl.when(near)
    def _():
        relay_pieces()

    for turn in range(shares):
        for re in range(1, enc_size):
            for rb in range(inner):
                block = block_at(turn, (e + re) % enc_size, (b + rb) % inner)
                wait(kv_all.at[block], kv_rs.at[block])
    for share in range(shares):
        wait(q_all.at[share], q_rs.at[share])

    limit = limit_ref[0]
    scale_factor = HEAD_DIM ** (-0.5)
    key_count = seq_size * rows

    def attend(query):
        keys_flat = kv_all[:, 0].reshape(key_count, HEAD_DIM)
        values_flat = kv_all[:, 1].reshape(key_count, HEAD_DIM)
        scores = lax.dot_general(
            query, keys_flat, (((1,), (1,)), ((), ())), preferred_element_type=jnp.float32
        ) * scale_factor
        position = lax.broadcasted_iota(jnp.int32, scores.shape, 1)
        masked = jnp.where(position < limit, scores, lowest_score)
        weights = jnp.exp(masked - jnp.max(masked, axis=1, keepdims=True))
        mass = jnp.sum(weights, axis=1, keepdims=True)
        mixed = jnp.dot(
            weights.astype(jnp.bfloat16), values_flat, preferred_element_type=jnp.float32
        )
        return (mixed / mass).astype(jnp.bfloat16)

    mine = h * enc_size + a // 2
    which = a % 2
    for turn in range(shares):
        share = share_of(turn + 1)
        plane = share * enc_size + e
        att_send[turn] = attend(q_all[share])

        @pl.when(plane == a)
        def _():
            pltpu.make_async_copy(
                att_send.at[turn], att_all.at[mine, which], a_rs.at[mine, which]
            ).start()

        @pl.when(plane != a)
        def _():
            send(
                att_send.at[turn], att_all.at[mine, which], a1_ss.at[turn],
                a_rs.at[mine, which], plane * inner + b, g,
            )

        if turn == 0:
            for r in range(1, outer_half):
                x = (line_peer(r) + outer_half) % outer
                wait(w_line.at[x], wl_rs.at[x])
                spread_piece(w_line.at[x], outer_half + r, x)

            @pl.when(jnp.logical_not(near))
            def _():
                relay_pieces()

    @pl.when(e == catcher)
    def _():
        for ra in range(outer):
            plane = (a + ra) % outer
            group, i = h * enc_size + plane // 2, plane % 2
            wait(att_all.at[group, i], a_rs.at[group, i])
            for r in range(1, groups):
                send(
                    att_all.at[group, i], att_all.at[group, i], a2_ss.at[ra, r],
                    a_rs.at[group, i], s, group_peer(r),
                )
        for rh in range(enc_size, groups):
            group = (h * enc_size + rh) % groups
            for i in range(2):
                wait(att_all.at[group, i], a_rs.at[group, i])

    @pl.when(e != catcher)
    def _():
        for group in range(groups):
            for i in range(2):
                wait(att_all.at[group, i], a_rs.at[group, i])

    width = w_ref.shape[1]
    for piece in range(inner):
        summed = None
        for group in range(groups):
            relayed = jnp.logical_and(
                piece == b, by_relay(group // enc_size, group % enc_size, h)
            )

            @pl.when(jnp.logical_not(relayed))
            def _():
                wait(w_all.at[piece, group], w2_rs.at[piece, group])

            lhs = jnp.concatenate([att_all[group, 0], att_all[group, 1]], axis=1)
            term = jnp.dot(lhs, w_all[piece, group], preferred_element_type=jnp.float32)
            term = term.astype(jnp.bfloat16).astype(jnp.float32)
            summed = term if summed is None else summed + term
        columns = slice(piece * width, (piece + 1) * width)
        out_ref[:, columns] = (gate_ref[columns][None, :] * summed).astype(jnp.bfloat16)

    for r in range(1, groups):
        wait(sums.at[g], sums_ss.at[r])
    for i in range(2):
        @pl.when(jnp.logical_not(jnp.logical_and(e * 2 + i == a, catcher == e)))
        def _():
            wait(kv_send.at[i], kv1_ss.at[i])
            wait(q_send.at[i], q1_ss.at[i])
    for turn in range(shares):
        for re in range(1, enc_size):
            wait(kv_send.at[0], kv2_ss.at[turn, re])
        for rb in range(1, inner):
            wait(kv_send.at[0], kv2_ss.at[turn, enc_size + rb])
            for re in range(1, enc_size):
                wait(kv_send.at[0], kv3_ss.at[turn, rb, re])

        @pl.when(share_of(turn + 1) * enc_size + e != a)
        def _():
            wait(att_send.at[turn], a1_ss.at[turn])

    @pl.when(e == catcher)
    def _():
        for ra in range(outer):
            for r in range(1, groups):
                wait(att_send.at[0], a2_ss.at[ra, r])

    for turn in range(2):
        for r in range(1, outer_half):
            wait(w_ref, wl_ss.at[turn, r])
    wait(w_ref, wl_ss.at[0, 0])
    pieces = [(0, a), (1, a_mirror)]
    for r in range(1, outer_half):
        pieces.append((1 + r, line_peer(r)))
        pieces.append((outer_half + r, (line_peer(r) + outer_half) % outer))
    for slot, x in pieces:
        for rb in range(inner):
            if rb == 0:
                @pl.when(x != g)
                def _():
                    wait(w_ref, w2_ss.at[slot, rb])
            else:
                @pl.when(jnp.logical_not(by_relay(h, e, x // enc_size)))
                def _():
                    wait(w_ref, w2_ss.at[slot, rb])
    for group in range(groups):
        @pl.when(by_relay(group // enc_size, group % enc_size, h))
        def _():
            for rb in range(1, inner):
                wait(w_ref, w3_ss.at[group, rb])


def fused(queries, keys, values, out_weight, q_gain, k_gain, gate, valid_count):
    seq_size = lax.axis_size("seq")
    groups = lax.axis_size("head") * lax.axis_size("enc")
    inner = seq_size // groups
    outer = seq_size // inner
    rows, local_width = queries.shape
    depth, width = out_weight.shape
    enc_size = lax.axis_size("enc")
    shares = outer // enc_size
    outer_half = outer // 2
    bf16, f32 = jnp.bfloat16, jnp.float32
    dma = pltpu.SemaphoreType.DMA
    vmem = pl.BlockSpec(memory_space=pltpu.VMEM)
    return pl.pallas_call(
        fused_kernel,
        out_shape=jax.ShapeDtypeStruct((rows, width * inner), bf16),
        in_specs=[pl.BlockSpec(memory_space=pltpu.SMEM)] + [vmem] * 7,
        out_specs=vmem,
        scratch_shapes=[
            pltpu.VMEM((groups, 16, rows), f32),
            pltpu.VMEM((2, 2, rows, HEAD_DIM), bf16),
            pltpu.VMEM((seq_size, 2, rows, HEAD_DIM), bf16),
            pltpu.VMEM((2, rows, HEAD_DIM), bf16),
            pltpu.VMEM((shares, rows, HEAD_DIM), bf16),
            pltpu.VMEM((outer, depth, width), bf16),
            pltpu.VMEM((inner, groups, depth, width), bf16),
            pltpu.VMEM((shares, rows, HEAD_DIM), bf16),
            pltpu.VMEM((groups, 2, rows, HEAD_DIM), bf16),
            dma((groups,)), dma((groups,)),
            dma((2,)), dma((2,)), dma((shares,)),
            dma((shares, enc_size + inner)), dma((shares, inner, enc_size)), dma((seq_size,)),
            dma((2, outer_half)), dma((outer,)),
            dma((outer, inner)), dma((inner, groups)), dma((groups, inner)),
            dma((shares,)), dma((outer, groups)), dma((groups, 2)),
        ],
        compiler_params=pltpu.CompilerParams(
            collective_id=0, has_side_effects=True, vmem_limit_bytes=56 * 2**20
        ),
    )(
        valid_count, queries, keys, values, out_weight,
        q_gain[None, :], k_gain[None, :], gate,
    )


def one_kernel_fits(mesh, queries, out_weight):
    sizes = mesh.shape
    seq_size, groups = sizes["seq"], sizes["head"] * sizes["enc"]
    return (
        seq_size % groups == 0
        and groups % 2 == 0
        and seq_size // (seq_size // groups) == 2 * sizes["enc"]
        and queries.shape[1] == 2 * groups * HEAD_DIM
        and (out_weight.shape[1] // seq_size) % HEAD_DIM == 0
    )


def solution(mesh):
    placed = (
        P("seq", ("head", "enc")),
        P("seq", ("head", "enc")),
        P("seq", ("head", "enc")),
        P(("head", "enc"), "seq"),
        P(("head", "enc")),
        P(("head", "enc")),
        P(("head", "enc")),
        P(),
    )

    def run(*arguments):
        body = fused if one_kernel_fits(mesh, arguments[0], arguments[3]) else local
        return jax.shard_map(
            body, mesh=mesh, in_specs=placed, out_specs=P("seq", ("head", "enc")),
            check_vma=False,
        )(*arguments)

    return run
```
